256 devices in a mesh: row: 16 (over x, z_hi), col: 16 (over y, z_lo, core).
Axes of the slice: x: 4, y: 4, z: 8 (z_hi: 4, z_lo: 2; z = z_hi * 2 + z_lo), core: 2. Of those that a mesh axis runs over, the one named last changes fastest.
Arguments:
- amplitudes: bfloat16 [1280, 32768], P('row', 'col'), may hold values from -6 to 6
- integrals: bfloat16 [32768, 16384], P('col', 'row'), may hold values from -0.046875 to 0.046875
Outputs:
- ladder: bfloat16 [16384, 1280], P(('row', 'col'))
The draws below stay inside these ranges and needn't reach their ends.
All inputs are finite; a program needn't handle non-finite values.
Results may differ from the reference program's by a relative error of at most 0.001.
Values may be sent and summed in bfloat16 or wider, within the bound.
No kernel may reach another device: no remote copies, remote signals or barrier semaphores. Data moves between devices by JAX's collectives and lax.ppermute only.
A program may use at most 64 MiB of HBM per device.

```python
import jax
import jax.numpy as jnp
from jax import lax

OPAIRS = 1280
CD_DEV = 2048
AB_DEV = 1024
CD = 32768
AB = 16384
N_ROW = 16
N_COL = 16


def raised(entries, rng, source, target, parts, factor):
    def block_of(axis_at):
        return (jnp.arange(entries.shape[axis_at]) // (entries.shape[axis_at] // parts)).reshape((-1,) + (1,) * (entries.ndim - 1 - axis_at))

    near = jax.random.permutation(rng, parts)[block_of(target)]
    other_side = (block_of(target) + parts // 2) % parts
    return jnp.where((block_of(source) == near) | (block_of(source) == other_side), factor * entries, entries)


def levels(rng, dims, shards, smallest, high):
    level, own = 1.0, jax.random.fold_in(rng, 6)
    for position, blocks in shards:
        heights = jnp.exp(jax.random.uniform(jax.random.fold_in(own, position), (blocks,), jnp.float32, smallest / len(shards), high / len(shards)))
        level = level * jnp.repeat(heights, dims[position] // blocks).reshape([-1 if axis == position else 1 for axis in range(len(dims))])
    return level


def gaussian(rng, extent, scale, most, cuts=(), held_as=jnp.bfloat16):
    values = jax.random.normal(rng, extent, jnp.float32) * scale
    if len(cuts) > 0:
        values = levels(rng, extent, cuts, -0.22, 0.18) * values
    return jnp.clip(values, min=-most, max=most).astype(held_as)


def bell_draw_with(own_key, dims, spread, most, cuts, heavy, kind=jnp.bfloat16):
    drawn = spread * jax.random.normal(own_key, dims, jnp.float32)
    if cuts:
        drawn = drawn * levels(own_key, dims, cuts, -0.22, 0.18)
    return jnp.clip(raised(drawn, jax.random.fold_in(own_key, 3), *heavy), -most, most).astype(kind)


def setup_inputs(seed: int = 0) -> dict:
    key_of = jax.random.split(jax.random.key(seed), 3)
    return {
        "amplitudes": gaussian(key_of[0], (OPAIRS, CD), 1.0, 6.0, ((0, 16), (1, 16))),
        "integrals": bell_draw_with(key_of[1], (CD, AB), CD ** -0.5, 0.046875, ((0, 16), (1, 16)), (0, 1, 16, 2.0)),
    }


def reference(amplitudes, integrals):
    blocks_amp = amplitudes.reshape(OPAIRS, N_COL, CD_DEV).transpose(1, 0, 2)
    blocks_int = integrals.reshape(N_COL, CD_DEV, AB_DEV * N_ROW)

    def accumulate(total, pieces):
        amp_block, int_block = pieces
        return total + jnp.dot(amp_block, int_block, preferred_element_type=jnp.float32), None

    start = jnp.zeros((OPAIRS, AB_DEV * N_ROW), jnp.float32)
    total, _ = lax.scan(accumulate, start, (blocks_amp, blocks_int))
    return total.T.astype(jnp.bfloat16)
```

```python
import jax
import jax.numpy as jnp
from jax import lax
from jax.sharding import PartitionSpec as P


def local(amplitudes, integrals):
    gathered = lax.all_gather(amplitudes, "row", axis=0, tiled=True)
    partial_value = lax.dot_general(
        integrals, gathered, (((0,), (1,)), ((), ())), preferred_element_type=jnp.float32
    )
    summed = lax.psum_scatter(partial_value, "col", scatter_dimension=0, tiled=True)
    return summed.astype(jnp.bfloat16)


def solution(mesh):
    placed = (P("row", "col"), P("col", "row"))
    return jax.shard_map(
        local, mesh=mesh, in_specs=placed, out_specs=P(("row", "col"), None), check_vma=False
    )
```

```python
import jax
import jax.numpy as jnp
from jax import lax
from jax.sharding import Mesh, PartitionSpec as P

ROWS = 80
F32 = jnp.float32
BF16 = jnp.bfloat16


def shift(value, axis, size, by):
    return lax.ppermute(value, axis, [(i, (i + by) % size) for i in range(size)])


def near(block, axis):
    return shift(block, axis, 4, 1), shift(block, axis, 4, -1)


def opposite(before, after, axis):
    half = before.shape[0] // 2
    return shift(after[:half], axis, 4, -1), shift(before[half:], axis, 4, 1)


def local(amplitudes, integrals):
    x, zh, zl, core = (lax.axis_index(n) for n in ("x", "zh", "zl", "core"))

    out_col = lax.broadcasted_iota(jnp.int32, (1024, 1024), 1)
    in_col = lax.broadcasted_iota(jnp.int32, (1024, 1024), 0)
    owner = jnp.where(out_col < 512, 1 - core, core)
    inside = out_col % 512
    source = (inside // 64) * 128 + owner * 64 + inside % 64
    order = (in_col == source).astype(BF16)
    columns = jnp.dot(integrals, order, preferred_element_type=F32).astype(BF16)
    theirs, mine = columns[:, :512], columns[:, 512:]

    def reduced(rows):
        away = jnp.dot(rows, theirs, preferred_element_type=F32)
        kept = jnp.dot(rows, mine, preferred_element_type=F32)
        pair = kept + lax.ppermute(away, "core", [(0, 1), (1, 0)])
        split = pair.reshape(rows.shape[0], 4, 128).transpose(1, 0, 2)
        spread = lax.all_to_all(split, "y", split_axis=0, concat_axis=0, tiled=True)
        over_y = jnp.sum(spread, axis=0)
        total = over_y + lax.ppermute(over_y, "zl", [(0, 1), (1, 0)])
        return total.astype(BF16)

    def block(dx, dz, first=0, count=ROWS):
        start = (((x + dx) % 4) * 4 + (zh + dz) % 4) * ROWS + first
        return start + jnp.arange(count)

    own = amplitudes
    zm, zp = near(own, "zh")
    own_xm, own_xp = near(own, "x")
    own_far = opposite(own_xm, own_xp, "x")
    far = jnp.concatenate(opposite(zm, zp, "zh"), axis=0)
    side = jnp.concatenate([zm, zp], axis=0)
    side_xm, side_xp = near(side, "x")
    far_xm, far_xp = near(far, "x")
    side_far = opposite(side_xm, side_xp, "x")
    far_far = opposite(far_xm, far_xp, "x")

    def pair_at(dx):
        return [block(dx, -1), block(dx, 1)]

    groups = [
        ([own, own_xm, own_xp], [block(0, 0), block(-1, 0), block(1, 0)]),
        ([side, *own_far], [*pair_at(0), block(2, 0, 0, 40), block(2, 0, 40, 40)]),
        ([side_xm, side_xp, far], [*pair_at(-1), *pair_at(1), block(0, 2)]),
        ([far_xm, far_xp, *side_far], [block(-1, 2), block(1, 2), *pair_at(2)]),
        ([*far_far], [block(2, 2, 0, 40), block(2, 2, 40, 40)]),
    ]
    sums = [reduced(jnp.concatenate(parts, axis=0)) for parts, _ in groups]
    places = jnp.concatenate([p for _, ps in groups for p in ps])
    total = jnp.concatenate(sums, axis=0)
    place = (places[:, None] == jnp.arange(1280)[None, :]).astype(BF16)
    turned = lax.dot_general(total, place, (((0,), (0,)), ((), ())), preferred_element_type=F32)
    return lax.dynamic_slice_in_dim(turned, zl * 64, 64, axis=0).astype(BF16)


def solution(mesh):
    split = Mesh(mesh.devices.reshape(4, 4, 4, 2, 2), ("x", "zh", "y", "zl", "core"))
    row, col = ("x", "zh"), ("y", "zl", "core")
    return jax.shard_map(
        local,
        mesh=split,
        in_specs=(P(row, col), P(col, row)),
        out_specs=P(row + col, None),
        check_vma=False,
    )
```

```python
import jax
import jax.numpy as jnp
from jax import lax
from jax.sharding import Mesh, PartitionSpec as P

ROWS = 80
F32 = jnp.float32
BF16 = jnp.bfloat16


def shift(value, axis, size, by):
    return lax.ppermute(value, axis, [(i, (i + by) % size) for i in range(size)])


def to_both(value, axis):
    return shift(value, axis, 4, 1), shift(value, axis, 4, -1)


def swap(value, axis):
    return lax.ppermute(value, axis, [(0, 1), (1, 0)])


def joined(*parts):
    return jnp.concatenate(parts, axis=0)


def local(amplitudes, integrals):
    x, zh, y, zl, core = (lax.axis_index(n) for n in ("x", "zh", "y", "zl", "core"))

    out_col = lax.broadcasted_iota(jnp.int32, (1024, 1024), 1)
    in_col = lax.broadcasted_iota(jnp.int32, (1024, 1024), 0)
    owner = jnp.where(out_col < 512, 1 - core, core)
    level = jnp.where(out_col & 64 == 0, zl, 1 - zl)
    source = ((out_col >> 7) & 3) * 256 + level * 128 + owner * 64 + (out_col & 63)
    order = (in_col == source).astype(BF16)
    columns = jnp.dot(integrals, order, preferred_element_type=F32).astype(BF16)
    theirs, mine = columns[:, :512], columns[:, 512:]

    def paired(rows):
        away = swap(jnp.dot(rows, theirs, preferred_element_type=F32), "core")
        return jnp.dot(rows, mine, preferred_element_type=F32) + away

    def over_y(pair):
        split = pair.reshape(pair.shape[0], 4, 128).transpose(1, 0, 2)
        return jnp.sum(lax.all_to_all(split, "y", split_axis=0, concat_axis=0, tiled=True), axis=0)

    def over_y_at_once(pair):
        part = lambda d: lax.dynamic_slice_in_dim(pair, ((y + d) % 4) * 128, 128, axis=1)
        others = [shift(part(d), "y", 4, d) for d in (1, 3, 2)]
        return part(0) + others[0] + others[1] + others[2]

    def over_zl(some):
        return (some[:, :64] + swap(some, "zl")[:, 64:]).astype(BF16)

    def block(dx, dz, first=0, count=ROWS):
        start = (((x + dx) % 4) * 4 + (zh + dz) % 4) * ROWS + first
        return start + jnp.arange(count)

    own = amplitudes
    zm, zp = to_both(own, "zh")
    own_xm, own_xp = to_both(own, "x")
    side = joined(zm, zp)
    side_xm, side_xp = to_both(side, "x")
    far = joined(shift(zp[:40], "zh", 4, -1), shift(zm[40:], "zh", 4, 1))
    first = paired(joined(own, own_xm, own_xp, side))
    after_xm, after_xp, first = lax.optimization_barrier(
        (joined(far, own_xm[40:]), joined(far, own_xp[:40]), first)
    )
    from_xm, from_xp = shift(after_xm, "x", 4, 1), shift(after_xp, "x", 4, -1)
    second = paired(joined(side_xm, side_xp, far))
    after_xm, after_xp, second = lax.optimization_barrier(
        (joined(side_xm[80:], from_xm[40:80]), joined(side_xp[:80], from_xp[:40]), second)
    )
    last_xm, last_xp = shift(after_xm, "x", 4, 1), shift(after_xp, "x", 4, -1)
    third = paired(joined(from_xm, from_xp))
    last_xm, last_xp, third = lax.optimization_barrier((last_xm, last_xp, third))
    fourth = paired(joined(last_xm, last_xp))

    sums = [over_zl(over_y(pair)) for pair in (first, second, third)]
    sums.append(over_zl(over_y_at_once(fourth)))
    sites = [
        [block(0, 0), block(-1, 0), block(1, 0), block(0, -1), block(0, 1)],
        [block(-1, -1), block(-1, 1), block(1, -1), block(1, 1), block(0, 2)],
        [block(-1, 2), block(2, 0, 40, 40), block(1, 2), block(2, 0, 0, 40)],
        [block(2, 1), block(2, 2, 40, 40), block(2, -1), block(2, 2, 0, 40)],
    ]
    places = joined(*[p for ps in sites for p in ps])
    place = (places[:, None] == jnp.arange(1280)[None, :]).astype(BF16)
    turned = lax.dot_general(
        joined(*sums), place, (((0,), (0,)), ((), ())), preferred_element_type=F32
    )
    return turned.astype(BF16)


def solution(mesh):
    split = Mesh(mesh.devices.reshape(4, 4, 4, 2, 2), ("x", "zh", "y", "zl", "core"))
    row, col = ("x", "zh"), ("y", "zl", "core")
    return jax.shard_map(
        local,
        mesh=split,
        in_specs=(P(row, col), P(col, row)),
        out_specs=P(row + col, None),
        check_vma=False,
    )
```

```python
import jax
import jax.numpy as jnp
from jax import lax
from jax.sharding import Mesh, PartitionSpec as P

ROWS = 80
F32 = jnp.float32
BF16 = jnp.bfloat16


def shift(value, axis, size, by):
    return lax.ppermute(value, axis, [(i, (i + by) % size) for i in range(size)])


def to_both(value, axis):
    return shift(value, axis, 4, 1), shift(value, axis, 4, -1)


def swap(value, axis):
    return lax.ppermute(value, axis, [(0, 1), (1, 0)])


def dot(left, right):
    return jnp.dot(left, right, preferred_element_type=F32)


def joined(*parts):
    return jnp.concatenate(parts, axis=0)


def local(amplitudes, integrals):
    x, zh, y, zl, core = (lax.axis_index(n) for n in ("x", "zh", "y", "zl", "core"))

    at = jnp.arange(1024)
    owner = jnp.where(at < 512, 1 - core, core)
    level = jnp.where(at & 64 == 0, zl, 1 - zl)
    source = ((at >> 7) & 3) * 256 + level * 128 + owner * 64 + (at & 63)

    def over_y(pair):
        split = pair.reshape(pair.shape[0], 4, 128).transpose(1, 0, 2)
        return jnp.sum(lax.all_to_all(split, "y", split_axis=0, concat_axis=0, tiled=True), axis=0)

    def over_y_at_once(pair):
        part = lambda d: lax.dynamic_slice_in_dim(pair, ((y + d) % 4) * 128, 128, axis=1)
        others = [shift(part(d), "y", 4, d) for d in (1, 3, 2)]
        return part(0) + others[0] + others[1] + others[2]

    def over_zl(some):
        return (some[:, :64] + swap(some, "zl")[:, 64:]).astype(BF16)

    def block(dx, dz, first=0, count=ROWS):
        start = (((x + dx) % 4) * 4 + (zh + dz) % 4) * ROWS + first
        return start + jnp.arange(count)

    own = amplitudes
    zm, zp = to_both(own, "zh")
    own, source = lax.optimization_barrier((own, source))
    order = (jnp.arange(1024)[:, None] == source[None, :]).astype(BF16)
    columns = dot(integrals, order).astype(BF16)
    own_xm, own_xp = to_both(own, "x")
    theirs, mine = columns[:, :512], columns[:, 512:]

    side = joined(zm, zp)
    side_xm, side_xp = to_both(side, "x")
    far = joined(shift(zp[:40], "zh", 4, -1), shift(zm[40:], "zh", 4, 1))
    early = joined(own, own_xm, own_xp, side)
    early_sum = dot(early, mine) + swap(dot(early, theirs), "core")

    late = joined(side_xm, side_xp)
    after_xm, after_xp, early_sum, away = lax.optimization_barrier(
        (joined(far, own_xm[40:]), joined(far, own_xp[:40]), early_sum, dot(late, theirs))
    )
    from_xm, from_xp = shift(after_xm, "x", 4, 1), shift(after_xp, "x", 4, -1)
    away = joined(swap(away[:160], "core"), swap(away[160:], "core"))
    late_sum = dot(late, mine) + away
    after_xm, after_xp, early_sum, late_sum = lax.optimization_barrier(
        (joined(side_xm[80:], from_xm[40:80]), joined(side_xp[:80], from_xp[:40]), early_sum, late_sum)
    )
    last_xm, last_xp = shift(after_xm, "x", 4, 1), shift(after_xp, "x", 4, -1)
    rows = joined(far, from_xm, from_xp)
    second = dot(rows, mine) + swap(dot(rows, theirs), "core")
    last_xm, last_xp, second = lax.optimization_barrier((last_xm, last_xp, second))
    rows = joined(last_xm, last_xp)
    third = dot(rows, mine) + swap(dot(rows, theirs), "core")

    sums = [over_zl(over_y(pair)) for pair in (joined(early_sum, late_sum), second)]
    sums.append(over_zl(over_y_at_once(third)))
    sites = [
        [block(0, 0), block(-1, 0), block(1, 0), block(0, -1), block(0, 1)],
        [block(-1, -1), block(-1, 1), block(1, -1), block(1, 1)],
        [block(0, 2), block(-1, 2), block(2, 0, 40, 40), block(1, 2), block(2, 0, 0, 40)],
        [block(2, 1), block(2, 2, 40, 40), block(2, -1), block(2, 2, 0, 40)],
    ]
    places = joined(*[p for ps in sites for p in ps])
    place = (places[:, None] == jnp.arange(1280)[None, :]).astype(BF16)
    turned = lax.dot_general(
        joined(*sums), place, (((0,), (0,)), ((), ())), preferred_element_type=F32
    )
    return turned.astype(BF16)


def solution(mesh):
    split = Mesh(mesh.devices.reshape(4, 4, 4, 2, 2), ("x", "zh", "y", "zl", "core"))
    row, col = ("x", "zh"), ("y", "zl", "core")
    return jax.shard_map(
        local,
        mesh=split,
        in_specs=(P(row, col), P(col, row)),
        out_specs=P(row + col, None),
        check_vma=False,
    )
```

```python
import jax
import jax.numpy as jnp
from jax import lax
from jax.sharding import Mesh, PartitionSpec as P

ROWS = 80
F32 = jnp.float32
BF16 = jnp.bfloat16


def shift(value, axis, size, by):
    return lax.ppermute(value, axis, [(i, (i + by) % size) for i in range(size)])


def to_both(value, axis):
    return shift(value, axis, 4, 1), shift(value, axis, 4, -1)


def swap(value, axis):
    return lax.ppermute(value, axis, [(0, 1), (1, 0)])


def dot(left, right):
    return jnp.dot(left, right, preferred_element_type=F32)


def joined(*parts):
    return jnp.concatenate(parts, axis=0)


def local(amplitudes, integrals):
    x, zh, y, zl, core = (lax.axis_index(n) for n in ("x", "zh", "y", "zl", "core"))

    at = jnp.arange(1024)
    owner = jnp.where(at < 512, 1 - core, core)
    level = jnp.where(at & 64 == 0, zl, 1 - zl)
    source = ((at >> 7) & 3) * 256 + level * 128 + owner * 64 + (at & 63)

    def over_y(pair):
        split = pair.reshape(pair.shape[0], 4, 128).transpose(1, 0, 2)
        return jnp.sum(lax.all_to_all(split, "y", split_axis=0, concat_axis=0, tiled=True), axis=0)

    def over_y_at_once(pair):
        part = lambda d: lax.dynamic_slice_in_dim(pair, ((y + d) % 4) * 128, 128, axis=1)
        others = [shift(part(d), "y", 4, d) for d in (1, 3, 2)]
        return part(0) + others[0] + others[1] + others[2]

    def over_zl(some):
        return (some[:, :64] + swap(some, "zl")[:, 64:]).astype(BF16)

    def block(dx, dz, first=0, count=ROWS):
        start = (((x + dx) % 4) * 4 + (zh + dz) % 4) * ROWS + first
        return start + jnp.arange(count)

    own = amplitudes
    zm, zp = to_both(own, "zh")
    own_xm, own_xp = to_both(own, "x")
    order = (jnp.arange(1024)[:, None] == source[None, :]).astype(BF16)
    columns = dot(integrals, order).astype(BF16)
    theirs, mine = columns[:, :512], columns[:, 512:]

    def paired(rows):
        return dot(rows, mine) + swap(dot(rows, theirs), "core")

    side, own_xm, own_xp = lax.optimization_barrier((joined(zm, zp), own_xm, own_xp))
    side_xm, side_xp = to_both(side, "x")
    far = joined(shift(zp[:40], "zh", 4, -1), shift(zm[40:], "zh", 4, 1))
    early = paired(joined(own, own_xm, own_xp, side))

    after_xm, after_xp, early = lax.optimization_barrier(
        (joined(far, own_xm[40:]), joined(far, own_xp[:40]), early)
    )
    from_xm, from_xp = shift(after_xm, "x", 4, 1), shift(after_xp, "x", 4, -1)
    side_xm, side_xp, early = lax.optimization_barrier((side_xm, side_xp, early))
    early = over_y(early)
    late = paired(joined(side_xm, side_xp))
    from_xm, from_xp, late = lax.optimization_barrier((from_xm, from_xp, late))
    after_xm, after_xp, early = lax.optimization_barrier(
        (joined(side_xm[80:], from_xm[40:80]), joined(side_xp[:80], from_xp[:40]), early)
    )
    last_xm, last_xp = shift(after_xm, "x", 4, 1), shift(after_xp, "x", 4, -1)
    late = over_y(late)
    second = paired(joined(far, from_xm, from_xp))
    last_xm, last_xp, second = lax.optimization_barrier((last_xm, last_xp, second))
    second = over_y(second)
    third = over_y_at_once(paired(joined(last_xm, last_xp)))
    sums = [over_zl(part) for part in (joined(early, late), second, third)]
    sites = [
        [block(0, 0), block(-1, 0), block(1, 0), block(0, -1), block(0, 1)],
        [block(-1, -1), block(-1, 1), block(1, -1), block(1, 1)],
        [block(0, 2), block(-1, 2), block(2, 0, 40, 40), block(1, 2), block(2, 0, 0, 40)],
        [block(2, 1), block(2, 2, 40, 40), block(2, -1), block(2, 2, 0, 40)],
    ]
    places = joined(*[p for ps in sites for p in ps])
    place = (places[:, None] == jnp.arange(1280)[None, :]).astype(BF16)
    turned = lax.dot_general(
        joined(*sums), place, (((0,), (0,)), ((), ())), preferred_element_type=F32
    )
    return turned.astype(BF16)


def solution(mesh):
    split = Mesh(mesh.devices.reshape(4, 4, 4, 2, 2), ("x", "zh", "y", "zl", "core"))
    row, col = ("x", "zh"), ("y", "zl", "core")
    return jax.shard_map(
        local,
        mesh=split,
        in_specs=(P(row, col), P(col, row)),
        out_specs=P(row + col, None),
        check_vma=False,
    )
```

```python
import jax
import jax.numpy as jnp
from jax import lax
from jax.sharding import Mesh, PartitionSpec as P

ROWS = 80
F32 = jnp.float32
BF16 = jnp.bfloat16


def shift(value, axis, size, by):
    return lax.ppermute(value, axis, [(i, (i + by) % size) for i in range(size)])


def to_both(value, axis):
    return shift(value, axis, 4, 1), shift(value, axis, 4, -1)


def swap(value, axis):
    return lax.ppermute(value, axis, [(0, 1), (1, 0)])


def dot(left, right):
    return jnp.dot(left, right, preferred_element_type=F32)


def joined(*parts):
    return jnp.concatenate(parts, axis=0)


def local(amplitudes, integrals):
    x, zh, y, zl, core = (lax.axis_index(n) for n in ("x", "zh", "y", "zl", "core"))

    at = jnp.arange(1024)
    owner = jnp.where(at < 512, 1 - core, core)
    level = jnp.where(at & 64 == 0, zl, 1 - zl)
    source = ((at >> 7) & 3) * 256 + level * 128 + owner * 64 + (at & 63)

    def over_y(pair):
        split = pair.reshape(pair.shape[0], 4, 128).transpose(1, 0, 2)
        return jnp.sum(lax.all_to_all(split, "y", split_axis=0, concat_axis=0, tiled=True), axis=0)

    def over_y_at_once(pair):
        part = lambda d: lax.dynamic_slice_in_dim(pair, ((y + d) % 4) * 128, 128, axis=1)
        others = [shift(part(d), "y", 4, d) for d in (1, 3, 2)]
        return part(0) + others[0] + others[1] + others[2]

    def over_zl(some):
        return (some[:, :64] + swap(some, "zl")[:, 64:]).astype(BF16)

    def block(dx, dz, first=0, count=ROWS):
        start = (((x + dx) % 4) * 4 + (zh + dz) % 4) * ROWS + first
        return start + jnp.arange(count)

    own = amplitudes
    zm, zp = to_both(own, "zh")
    own_xm, own_xp = to_both(own, "x")
    order = (jnp.arange(1024)[:, None] == source[None, :]).astype(BF16)
    columns = dot(integrals, order).astype(BF16)
    theirs, mine = columns[:, :512], columns[:, 512:]

    def paired(rows):
        return dot(rows, mine) + swap(dot(rows, theirs), "core")

    side = joined(zm, zp)
    side_xm, side_xp = to_both(side, "x")
    far = joined(shift(zp[:40], "zh", 4, -1), shift(zm[40:], "zh", 4, 1))
    early = paired(joined(own, *lax.optimization_barrier((own_xm, own_xp, side))))

    late_rows = joined(side_xm, side_xp)
    after_xm, after_xp, early, away = lax.optimization_barrier(
        (joined(far, own_xm[40:]), joined(far, own_xp[:40]), early, dot(late_rows, theirs))
    )
    from_xm, from_xp = shift(after_xm, "x", 4, 1), shift(after_xp, "x", 4, -1)
    early = over_y(early)
    late = dot(late_rows, mine) + joined(swap(away[:160], "core"), swap(away[160:], "core"))
    from_xm, from_xp, late = lax.optimization_barrier((from_xm, from_xp, late))
    after_xm, after_xp, early = lax.optimization_barrier(
        (joined(side_xm[80:], from_xm[40:80]), joined(side_xp[:80], from_xp[:40]), early)
    )
    last_xm, last_xp = shift(after_xm, "x", 4, 1), shift(after_xp, "x", 4, -1)
    second = paired(joined(far, from_xm, from_xp))
    last_xm, last_xp, second = lax.optimization_barrier((last_xm, last_xp, second))
    second = over_y(joined(late, second))
    third = over_y_at_once(paired(joined(last_xm, last_xp)))
    sums = [over_zl(part) for part in (early, second, third)]
    sites = [
        [block(0, 0), block(-1, 0), block(1, 0), block(0, -1), block(0, 1)],
        [block(-1, -1), block(-1, 1), block(1, -1), block(1, 1)],
        [block(0, 2), block(-1, 2), block(2, 0, 40, 40), block(1, 2), block(2, 0, 0, 40)],
        [block(2, 1), block(2, 2, 40, 40), block(2, -1), block(2, 2, 0, 40)],
    ]
    places = joined(*[p for ps in sites for p in ps])
    place = (places[:, None] == jnp.arange(1280)[None, :]).astype(BF16)
    turned = lax.dot_general(
        joined(*sums), place, (((0,), (0,)), ((), ())), preferred_element_type=F32
    )
    return turned.astype(BF16)


def solution(mesh):
    split = Mesh(mesh.devices.reshape(4, 4, 4, 2, 2), ("x", "zh", "y", "zl", "core"))
    row, col = ("x", "zh"), ("y", "zl", "core")
    return jax.shard_map(
        local,
        mesh=split,
        in_specs=(P(row, col), P(col, row)),
        out_specs=P(row + col, None),
        check_vma=False,
    )
```

```python
import jax
import jax.numpy as jnp
from jax import lax
from jax.sharding import Mesh, PartitionSpec as P

ROWS = 80
F32 = jnp.float32
BF16 = jnp.bfloat16


def shift(value, axis, size, by):
    return lax.ppermute(value, axis, [(i, (i + by) % size) for i in range(size)])


def to_both(value, axis):
    return shift(value, axis, 4, 1), shift(value, axis, 4, -1)


def swap(value, axis):
    return lax.ppermute(value, axis, [(0, 1), (1, 0)])


def dot(left, right):
    return jnp.dot(left, right, preferred_element_type=F32)


def joined(*parts):
    return jnp.concatenate(parts, axis=0)


def local(amplitudes, integrals):
    x, zh, y, zl, core = (lax.axis_index(n) for n in ("x", "zh", "y", "zl", "core"))

    at = jnp.arange(1024)
    owner = jnp.where(at < 512, 1 - core, core)
    level = jnp.where(at & 64 == 0, zl, 1 - zl)
    source = ((at >> 7) & 3) * 256 + level * 128 + owner * 64 + (at & 63)

    def over_y(pair):
        split = pair.reshape(pair.shape[0], 4, 128).transpose(1, 0, 2)
        return jnp.sum(lax.all_to_all(split, "y", split_axis=0, concat_axis=0, tiled=True), axis=0)

    def over_y_at_once(pair):
        part = lambda d: lax.dynamic_slice_in_dim(pair, ((y + d) % 4) * 128, 128, axis=1)
        others = [shift(part(d), "y", 4, d) for d in (1, 3, 2)]
        return part(0) + others[0] + others[1] + others[2]

    def over_zl(some):
        return (some[:, :64] + swap(some, "zl")[:, 64:]).astype(BF16)

    def block(dx, dz, first=0, count=ROWS):
        start = (((x + dx) % 4) * 4 + (zh + dz) % 4) * ROWS + first
        return start + jnp.arange(count)

    own = amplitudes
    zm, zp = to_both(own, "zh")
    own_xm, own_xp = to_both(own, "x")
    order = (jnp.arange(1024)[:, None] == source[None, :]).astype(BF16)
    columns = dot(integrals, order).astype(BF16)
    theirs, mine = columns[:, :512], columns[:, 512:]

    def paired(rows):
        return dot(rows, mine) + swap(dot(rows, theirs), "core")

    side = joined(zm, zp)
    side_xm, side_xp = to_both(side, "x")
    far = joined(shift(zp[:40], "zh", 4, -1), shift(zm[40:], "zh", 4, 1))
    early = paired(joined(own, *lax.optimization_barrier((own_xm, own_xp, side))))

    late_rows = joined(side_xm, side_xp)
    after_xm, after_xp, early, away = lax.optimization_barrier(
        (joined(far, own_xm[40:]), joined(far, own_xp[:40]), early, dot(late_rows, theirs))
    )
    from_xm, from_xp = shift(after_xm, "x", 4, 1), shift(after_xp, "x", 4, -1)
    early = over_y(early)
    kept_rows, early = lax.optimization_barrier((late_rows, early))
    late = dot(kept_rows, mine) + joined(swap(away[:160], "core"), swap(away[160:], "core"))
    from_xm, from_xp, late = lax.optimization_barrier((from_xm, from_xp, late))
    last_xm = shift(joined(side_xm[80:], from_xm[40:80]), "x", 4, 1)
    last_xp = shift(joined(side_xp[:80], from_xp[:40]), "x", 4, -1)
    late = over_y(late)
    rows = joined(far, from_xm, from_xp)
    away = swap(dot(rows, theirs), "core")
    rows, late = lax.optimization_barrier((rows, late))
    second = dot(rows, mine) + away
    last_xm, last_xp, second = lax.optimization_barrier((last_xm, last_xp, second))
    second = over_y(second)
    third, second = lax.optimization_barrier((paired(joined(last_xm, last_xp)), second))
    third = over_y_at_once(third)
    sums = [over_zl(part) for part in (joined(early, late), second, third)]
    sites = [
        [block(0, 0), block(-1, 0), block(1, 0), block(0, -1), block(0, 1)],
        [block(-1, -1), block(-1, 1), block(1, -1), block(1, 1)],
        [block(0, 2), block(-1, 2), block(2, 0, 40, 40), block(1, 2), block(2, 0, 0, 40)],
        [block(2, 1), block(2, 2, 40, 40), block(2, -1), block(2, 2, 0, 40)],
    ]
    places = joined(*[p for ps in sites for p in ps])
    place = (places[:, None] == jnp.arange(1280)[None, :]).astype(BF16)
    turned = lax.dot_general(
        joined(*sums), place, (((0,), (0,)), ((), ())), preferred_element_type=F32
    )
    return turned.astype(BF16)


def solution(mesh):
    split = Mesh(mesh.devices.reshape(4, 4, 4, 2, 2), ("x", "zh", "y", "zl", "core"))
    row, col = ("x", "zh"), ("y", "zl", "core")
    return jax.shard_map(
        local,
        mesh=split,
        in_specs=(P(row, col), P(col, row)),
        out_specs=P(row + col, None),
        check_vma=False,
    )
```

```python
import jax
import jax.numpy as jnp
from jax import lax
from jax.experimental import pallas as pl
from jax.experimental.pallas import tpu as pltpu
from jax.sharding import Mesh, PartitionSpec as P

ROWS = 80
F32 = jnp.float32
BF16 = jnp.bfloat16


def shift(value, axis, size, by):
    return lax.ppermute(value, axis, [(i, (i + by) % size) for i in range(size)])


def to_both(value, axis):
    return shift(value, axis, 4, 1), shift(value, axis, 4, -1)


def swap(value, axis):
    return lax.ppermute(value, axis, [(0, 1), (1, 0)])


def dot(left, right):
    return jnp.dot(left, right, preferred_element_type=F32)


def joined(*parts):
    return jnp.concatenate(parts, axis=0)


def product(parts, values, away=None):
    rows = sum(part.shape[0] for part in parts)
    depth = values.shape[0]

    def kernel(*refs):
        held, out = refs[-1], refs[-2]

        @pl.when(pl.program_id(0) == 0)
        def _():
            at = 0
            for ref in refs[: len(parts)]:
                held[at : at + ref.shape[0]] = ref[...]
                at += ref.shape[0]

        found = jnp.dot(held[...], refs[len(parts)][...], preferred_element_type=F32)
        if away is None:
            out[...] = found
        else:
            found += refs[len(parts) + 1][...]
            out[0], out[1] = found[:, :128], found[:, 128:]

    first = 0 if away is None else 2
    whole = [pl.BlockSpec(part.shape, lambda i: (0, 0)) for part in parts]
    half = pl.BlockSpec((rows, 256), lambda i: (0, i))
    split = pl.BlockSpec((2, rows, 128), lambda i: (i, 0, 0))
    return pl.pallas_call(
        kernel,
        grid=(2,),
        in_specs=whole + [pl.BlockSpec((depth, 256), lambda i: (0, i + first))] + ([] if away is None else [half]),
        out_specs=half if away is None else split,
        out_shape=jax.ShapeDtypeStruct((rows, 512) if away is None else (4, rows, 128), F32),
        scratch_shapes=[pltpu.VMEM((rows, depth), BF16)],
        cost_estimate=pl.CostEstimate(flops=0, bytes_accessed=0, transcendentals=0),
    )(*parts, values, *([] if away is None else [away]))


def local(amplitudes, integrals):
    x, zh, y, zl, core = (lax.axis_index(n) for n in ("x", "zh", "y", "zl", "core"))

    at = jnp.arange(1024)
    owner = jnp.where(at < 512, 1 - core, core)
    level = jnp.where(at & 64 == 0, zl, 1 - zl)
    source = ((at >> 7) & 3) * 256 + level * 128 + owner * 64 + (at & 63)

    def over_y(split):
        return jnp.sum(lax.all_to_all(split, "y", split_axis=0, concat_axis=0, tiled=True), axis=0)

    def over_y_at_once(split):
        part = lambda d: lax.dynamic_index_in_dim(split, (y + d) % 4, 0, keepdims=False)
        others = [shift(part(d), "y", 4, d) for d in (1, 3, 2)]
        return part(0) + others[0] + others[1] + others[2]

    def over_zl(some):
        return (some[:, :64] + swap(some, "zl")[:, 64:]).astype(BF16)

    def block(dx, dz, first=0, count=ROWS):
        start = (((x + dx) % 4) * 4 + (zh + dz) % 4) * ROWS + first
        return start + jnp.arange(count)

    own = amplitudes
    zm, zp = to_both(own, "zh")
    own_xm, own_xp = to_both(own, "x")
    order = (jnp.arange(1024)[:, None] == source[None, :]).astype(BF16)
    columns = dot(integrals, order).astype(BF16)

    def swapped(*parts):
        return swap(product(parts, columns), "core")

    side = joined(zm, zp)
    side_xm, side_xp = to_both(side, "x")
    far = joined(shift(zp[:40], "zh", 4, -1), shift(zm[40:], "zh", 4, 1))
    parts = (own, *lax.optimization_barrier((own_xm, own_xp, side)))
    early = product(parts, columns, swapped(*parts))

    after_xm, after_xp, early, away = lax.optimization_barrier(
        (joined(far, own_xm[40:]), joined(far, own_xp[:40]), early, product((side_xm, side_xp), columns))
    )
    from_xm, from_xp = shift(after_xm, "x", 4, 1), shift(after_xp, "x", 4, -1)
    early = over_y(early)
    late = product((side_xm, side_xp), columns, swap(away, "core"))
    from_xm, from_xp, late = lax.optimization_barrier((from_xm, from_xp, late))
    late = over_y_at_once(late)
    after_xm, after_xp, early = lax.optimization_barrier(
        (joined(side_xm[80:], from_xm[40:80]), joined(side_xp[:80], from_xp[:40]), early)
    )
    last_xm, last_xp = shift(after_xm, "x", 4, 1), shift(after_xp, "x", 4, -1)
    parts = (far, from_xm, from_xp)
    away, late = lax.optimization_barrier((swapped(*parts), late))
    second = product(parts, columns, away)
    last_xm, last_xp, second = lax.optimization_barrier((last_xm, last_xp, second))
    second = over_y(second)
    parts = (last_xm, last_xp)
    last = over_y_at_once(product(parts, columns, swapped(*parts)))
    sums = [over_zl(part) for part in (joined(early, late), second, last)]
    sites = [
        [block(0, 0), block(-1, 0), block(1, 0), block(0, -1), block(0, 1)],
        [block(-1, -1), block(-1, 1), block(1, -1), block(1, 1)],
        [block(0, 2), block(-1, 2), block(2, 0, 40, 40), block(1, 2), block(2, 0, 0, 40)],
        [block(2, 1), block(2, 2, 40, 40), block(2, -1), block(2, 2, 0, 40)],
    ]
    places = joined(*[p for ps in sites for p in ps])
    place = (places[:, None] == jnp.arange(1280)[None, :]).astype(BF16)
    turned = lax.dot_general(
        joined(*sums), place, (((0,), (0,)), ((), ())), preferred_element_type=F32
    )
    return turned.astype(BF16)


def solution(mesh):
    split = Mesh(mesh.devices.reshape(4, 4, 4, 2, 2), ("x", "zh", "y", "zl", "core"))
    row, col = ("x", "zh"), ("y", "zl", "core")
    return jax.shard_map(
        local,
        mesh=split,
        in_specs=(P(row, col), P(col, row)),
        out_specs=P(row + col, None),
        check_vma=False,
    )
```

```python
import jax
import jax.numpy as jnp
from jax import lax
from jax.sharding import Mesh, PartitionSpec as P

ROWS = 80
F32 = jnp.float32
BF16 = jnp.bfloat16


def shift(value, axis, size, by):
    return lax.ppermute(value, axis, [(i, (i + by) % size) for i in range(size)])


def to_both(value, axis):
    return shift(value, axis, 4, 1), shift(value, axis, 4, -1)


def swap(value, axis):
    return lax.ppermute(value, axis, [(0, 1), (1, 0)])


def dot(left, right):
    return jnp.dot(left, right, preferred_element_type=F32)


def joined(*parts):
    return jnp.concatenate(parts, axis=0)


def local(amplitudes, integrals):
    x, zh, y, zl, core = (lax.axis_index(n) for n in ("x", "zh", "y", "zl", "core"))

    at = jnp.arange(1024)
    owner = jnp.where(at < 512, 1 - core, core)
    level = jnp.where(at & 64 == 0, zl, 1 - zl)
    source = ((at >> 7) & 3) * 256 + level * 128 + owner * 64 + (at & 63)

    def over_y(pair):
        split = pair.reshape(pair.shape[0], 4, 128).transpose(1, 0, 2)
        return jnp.sum(lax.all_to_all(split, "y", split_axis=0, concat_axis=0, tiled=True), axis=0)

    def over_y_at_once(pair):
        part = lambda d: lax.dynamic_slice_in_dim(pair, ((y + d) % 4) * 128, 128, axis=1)
        others = [shift(part(d), "y", 4, d) for d in (1, 3, 2)]
        return part(0) + others[0] + others[1] + others[2]

    def over_zl(some):
        return (some[:, :64] + swap(some, "zl")[:, 64:]).astype(BF16)

    def block(dx, dz, first=0, count=ROWS):
        start = (((x + dx) % 4) * 4 + (zh + dz) % 4) * ROWS + first
        return start + jnp.arange(count)

    own = amplitudes
    zm, zp = to_both(own, "zh")
    own_xm, own_xp = to_both(own, "x")
    order = (jnp.arange(1024)[:, None] == source[None, :]).astype(BF16)
    columns = dot(integrals, order).astype(BF16)
    theirs, mine = columns[:, :512], columns[:, 512:]

    def paired(rows):
        return dot(rows, mine) + swap(dot(rows, theirs), "core")

    side = joined(zm, zp)
    side_xm, side_xp = to_both(side, "x")
    far = joined(shift(zp[:40], "zh", 4, -1), shift(zm[40:], "zh", 4, 1))
    early = paired(joined(own, *lax.optimization_barrier((own_xm, own_xp, side))))

    late_rows = joined(side_xm, side_xp)
    after_xm, after_xp, early, away = lax.optimization_barrier(
        (joined(far, own_xm[40:]), joined(far, own_xp[:40]), early, dot(late_rows, theirs))
    )
    from_xm, from_xp = shift(after_xm, "x", 4, 1), shift(after_xp, "x", 4, -1)
    late = dot(late_rows, mine) + swap(away, "core")
    early = over_y(joined(early, late))
    from_xm, from_xp, late = lax.optimization_barrier((from_xm, from_xp, late))
    last_xm = shift(joined(side_xm[80:], from_xm[40:80]), "x", 4, 1)
    last_xp = shift(joined(side_xp[:80], from_xp[:40]), "x", 4, -1)
    rows, early = lax.optimization_barrier((joined(far, from_xm, from_xp), early))
    away = dot(rows, theirs)
    away = joined(*[swap(piece, "core") for piece in (away[:104], away[104:208], away[208:])])
    second = dot(rows, mine) + away
    last_xm, last_xp, second = lax.optimization_barrier((last_xm, last_xp, second))
    second = over_y(second)
    third = over_y_at_once(paired(joined(last_xm, last_xp)))
    sums = [over_zl(part) for part in (early, second, third)]
    sites = [
        [block(0, 0), block(-1, 0), block(1, 0), block(0, -1), block(0, 1)],
        [block(-1, -1), block(-1, 1), block(1, -1), block(1, 1)],
        [block(0, 2), block(-1, 2), block(2, 0, 40, 40), block(1, 2), block(2, 0, 0, 40)],
        [block(2, 1), block(2, 2, 40, 40), block(2, -1), block(2, 2, 0, 40)],
    ]
    places = joined(*[p for ps in sites for p in ps])
    place = (places[:, None] == jnp.arange(1280)[None, :]).astype(BF16)
    turned = lax.dot_general(
        joined(*sums), place, (((0,), (0,)), ((), ())), preferred_element_type=F32
    )
    return turned.astype(BF16)


def solution(mesh):
    split = Mesh(mesh.devices.reshape(4, 4, 4, 2, 2), ("x", "zh", "y", "zl", "core"))
    row, col = ("x", "zh"), ("y", "zl", "core")
    return jax.shard_map(
        local,
        mesh=split,
        in_specs=(P(row, col), P(col, row)),
        out_specs=P(row + col, None),
        check_vma=False,
    )
```

```python
import jax
import jax.numpy as jnp
from jax import lax
from jax.sharding import Mesh, PartitionSpec as P

ROWS = 80
F32 = jnp.float32
BF16 = jnp.bfloat16


def shift(value, axis, size, by):
    return lax.ppermute(value, axis, [(i, (i + by) % size) for i in range(size)])


def to_both(value, axis):
    return shift(value, axis, 4, 1), shift(value, axis, 4, -1)


def swap(value, axis):
    return lax.ppermute(value, axis, [(0, 1), (1, 0)])


def dot(left, right):
    return jnp.dot(left, right, preferred_element_type=F32)


def joined(*parts):
    return jnp.concatenate(parts, axis=0)


def local(amplitudes, integrals):
    x, zh, y, zl, core = (lax.axis_index(n) for n in ("x", "zh", "y", "zl", "core"))

    at = jnp.arange(1024)
    owner = jnp.where(at < 512, 1 - core, core)
    level = jnp.where(at & 64 == 0, zl, 1 - zl)
    source = ((at >> 7) & 3) * 256 + level * 128 + owner * 64 + (at & 63)

    def over_y(pair):
        split = pair.reshape(pair.shape[0], 4, 128).transpose(1, 0, 2)
        return jnp.sum(lax.all_to_all(split, "y", split_axis=0, concat_axis=0, tiled=True), axis=0)

    def over_y_at_once(pair):
        part = lambda d: lax.dynamic_slice_in_dim(pair, ((y + d) % 4) * 128, 128, axis=1)
        others = [shift(part(d), "y", 4, d) for d in (1, 3, 2)]
        return part(0) + others[0] + others[1] + others[2]

    def over_zl(some):
        return (some[:, :64] + swap(some, "zl")[:, 64:]).astype(BF16)

    def block(dx, dz, first=0, count=ROWS):
        start = (((x + dx) % 4) * 4 + (zh + dz) % 4) * ROWS + first
        return start + jnp.arange(count)

    own = amplitudes
    zm, zp = to_both(own, "zh")
    own_xm, own_xp = to_both(own, "x")
    order = (jnp.arange(1024)[:, None] == source[None, :]).astype(BF16)
    columns = dot(integrals, order).astype(BF16)
    theirs, mine = columns[:, :512], columns[:, 512:]

    def paired(rows):
        return dot(rows, mine) + swap(dot(rows, theirs), "core")

    side = joined(zm, zp)
    side_xm, side_xp = to_both(side, "x")
    far = joined(shift(zp[:40], "zh", 4, -1), shift(zm[40:], "zh", 4, 1))
    early = paired(joined(own, *lax.optimization_barrier((own_xm, own_xp, side))))

    late_rows = joined(side_xm, side_xp)
    after_xm, after_xp, early, away = lax.optimization_barrier(
        (joined(far, own_xm[40:]), joined(far, own_xp[:40]), early, dot(late_rows, theirs))
    )
    from_xm, from_xp = shift(after_xm, "x", 4, 1), shift(after_xp, "x", 4, -1)
    late = dot(late_rows, mine) + swap(away, "core")
    early = over_y(joined(early, late))
    from_xm, from_xp, late = lax.optimization_barrier((from_xm, from_xp, late))
    last_xm = shift(joined(side_xm[80:], from_xm[40:80]), "x", 4, 1)
    last_xp = shift(joined(side_xp[:80], from_xp[:40]), "x", 4, -1)
    rows, early = lax.optimization_barrier((joined(far, from_xm, from_xp), early))
    away = dot(rows, theirs)
    away = joined(*[swap(piece, "core") for piece in (away[:104], away[104:208], away[208:])])
    second = dot(rows, mine) + away
    last_xm, last_xp, second = lax.optimization_barrier((last_xm, last_xp, second))
    second = over_y(second)
    third = over_y_at_once(paired(joined(last_xm, last_xp)))
    sums = [over_zl(part) for part in (early, second, third)]
    sites = [
        [block(0, 0), block(-1, 0), block(1, 0), block(0, -1), block(0, 1)],
        [block(-1, -1), block(-1, 1), block(1, -1), block(1, 1)],
        [block(0, 2), block(-1, 2), block(2, 0, 40, 40), block(1, 2), block(2, 0, 0, 40)],
        [block(2, 1), block(2, 2, 40, 40), block(2, -1), block(2, 2, 0, 40)],
    ]
    places = joined(*[p for ps in sites for p in ps])
    place = (places[:, None] == jnp.arange(1280)[None, :]).astype(BF16)

    def put(some, where):
        return lax.dot_general(some, where, (((0,), (0,)), ((), ())), preferred_element_type=F32)

    turned = put(joined(*sums[:2]), place[:1040]) + put(sums[2], place[1040:])
    return turned.astype(BF16)


def solution(mesh):
    split = Mesh(mesh.devices.reshape(4, 4, 4, 2, 2), ("x", "zh", "y", "zl", "core"))
    row, col = ("x", "zh"), ("y", "zl", "core")
    return jax.shard_map(
        local,
        mesh=split,
        in_specs=(P(row, col), P(col, row)),
        out_specs=P(row + col, None),
        check_vma=False,
    )
```

```python
import jax
import jax.numpy as jnp
from jax import lax
from jax.sharding import Mesh, PartitionSpec as P

ROWS = 80
F32 = jnp.float32
BF16 = jnp.bfloat16


def shift(value, axis, size, by):
    return lax.ppermute(value, axis, [(i, (i + by) % size) for i in range(size)])


def to_both(value, axis):
    return shift(value, axis, 4, 1), shift(value, axis, 4, -1)


def swap(value, axis):
    return lax.ppermute(value, axis, [(0, 1), (1, 0)])


def dot(left, right):
    return jnp.dot(left, right, preferred_element_type=F32)


def joined(*parts):
    return jnp.concatenate(parts, axis=0)


def local(amplitudes, integrals):
    x, zh, y, zl, core = (lax.axis_index(n) for n in ("x", "zh", "y", "zl", "core"))

    at = jnp.arange(1024)
    owner = jnp.where(at < 512, 1 - core, core)
    level = jnp.where(at & 64 == 0, zl, 1 - zl)
    source = ((at >> 7) & 3) * 256 + level * 128 + owner * 64 + (at & 63)

    def over_y(pair):
        split = pair.reshape(pair.shape[0], 4, 128).transpose(1, 0, 2)
        return jnp.sum(lax.all_to_all(split, "y", split_axis=0, concat_axis=0, tiled=True), axis=0)

    def over_y_at_once(pair):
        part = lambda d: lax.dynamic_slice_in_dim(pair, ((y + d) % 4) * 128, 128, axis=1)
        others = [shift(part(d), "y", 4, d) for d in (1, 3, 2)]
        return part(0) + others[0] + others[1] + others[2]

    def over_zl(some):
        return (some[:, :64] + swap(some, "zl")[:, 64:]).astype(BF16)

    def over_zl_folded(some):
        half = some.shape[0] // 2
        other = some[:, 64:]
        came = swap(jnp.concatenate([other[:half], other[half:]], axis=1), "zl")
        return (some[:, :64] + joined(came[:, :64], came[:, 64:])).astype(BF16)

    def block(dx, dz, first=0, count=ROWS):
        start = (((x + dx) % 4) * 4 + (zh + dz) % 4) * ROWS + first
        return start + jnp.arange(count)

    own = amplitudes
    zm, zp = to_both(own, "zh")
    own_xm, own_xp = to_both(own, "x")
    order = (jnp.arange(1024)[:, None] == source[None, :]).astype(BF16)
    columns = dot(integrals, order).astype(BF16)
    theirs, mine = columns[:, :512], columns[:, 512:]

    def paired(rows):
        return dot(rows, mine) + swap(dot(rows, theirs), "core")

    side = joined(zm, zp)
    side_xm, side_xp = to_both(side, "x")
    far = joined(shift(zp[:40], "zh", 4, -1), shift(zm[40:], "zh", 4, 1))
    early = paired(joined(own, *lax.optimization_barrier((own_xm, own_xp, side))))

    late_rows = joined(side_xm, side_xp)
    after_xm, after_xp, early, away = lax.optimization_barrier(
        (
            joined(far, own_xm[40:], side_xm[80:]),
            joined(far, own_xp[:40], side_xp[:80]),
            early,
            dot(late_rows, theirs),
        )
    )
    from_xm, from_xp = shift(after_xm, "x", 4, 1), shift(after_xp, "x", 4, -1)
    late = dot(late_rows, mine) + swap(away, "core")
    early = over_y(joined(early, late))
    from_xm, from_xp, late = lax.optimization_barrier((from_xm, from_xp, late))
    last_xm = shift(from_xm[40:80], "x", 4, 1)
    last_xp = shift(from_xp[:40], "x", 4, -1)
    rows, early = lax.optimization_barrier(
        (joined(far, from_xm, from_xp, last_xm, last_xp), early)
    )
    away = swap(dot(rows, theirs), "core")
    kept = lax.optimization_barrier(dot(rows, mine))
    last, early = lax.optimization_barrier((over_y_at_once(kept + away), over_zl(early)))
    sums = [early, over_zl_folded(last)]
    sites = [
        [block(0, 0), block(-1, 0), block(1, 0), block(0, -1), block(0, 1)],
        [block(-1, -1), block(-1, 1), block(1, -1), block(1, 1)],
        [block(0, 2), block(-1, 2), block(2, 0, 40, 40), block(2, 1)],
        [block(1, 2), block(2, 0, 0, 40), block(2, -1)],
        [block(2, 2, 40, 40), block(2, 2, 0, 40)],
    ]
    places = joined(*[p for ps in sites for p in ps])
    place = (places[:, None] == jnp.arange(1280)[None, :]).astype(BF16)

    def put(some, where):
        return lax.dot_general(some, where, (((0,), (0,)), ((), ())), preferred_element_type=F32)

    turned = put(sums[0], place[:720]) + put(sums[1], place[720:])
    return turned.astype(BF16)


def solution(mesh):
    split = Mesh(mesh.devices.reshape(4, 4, 4, 2, 2), ("x", "zh", "y", "zl", "core"))
    row, col = ("x", "zh"), ("y", "zl", "core")
    return jax.shard_map(
        local,
        mesh=split,
        in_specs=(P(row, col), P(col, row)),
        out_specs=P(row + col, None),
        check_vma=False,
    )
```

```python
import jax
import jax.numpy as jnp
from jax import lax
from jax.sharding import Mesh, PartitionSpec as P

ROWS = 80
F32 = jnp.float32
BF16 = jnp.bfloat16


def shift(value, axis, size, by):
    return lax.ppermute(value, axis, [(i, (i + by) % size) for i in range(size)])


def to_both(value, axis):
    return shift(value, axis, 4, 1), shift(value, axis, 4, -1)


def swap(value, axis):
    return lax.ppermute(value, axis, [(0, 1), (1, 0)])


def dot(left, right):
    return jnp.dot(left, right, preferred_element_type=F32)


def joined(*parts):
    return jnp.concatenate(parts, axis=0)


def local(amplitudes, integrals):
    x, zh, y, zl, core = (lax.axis_index(n) for n in ("x", "zh", "y", "zl", "core"))

    at = jnp.arange(1024)
    owner = jnp.where(at < 512, 1 - core, core)
    level = jnp.where(at & 64 == 0, zl, 1 - zl)
    source = ((at >> 7) & 3) * 256 + level * 128 + owner * 64 + (at & 63)

    def over_y(pair):
        split = pair.reshape(pair.shape[0], 4, 128).transpose(1, 0, 2)
        return jnp.sum(lax.all_to_all(split, "y", split_axis=0, concat_axis=0, tiled=True), axis=0)

    def over_y_at_once(pair):
        part = lambda d: lax.dynamic_slice_in_dim(pair, ((y + d) % 4) * 128, 128, axis=1)
        others = [shift(part(d), "y", 4, d) for d in (1, 3, 2)]
        return part(0) + others[0] + others[1] + others[2]

    def over_zl(some):
        return (some[:, :64] + swap(some, "zl")[:, 64:]).astype(BF16)

    def over_zl_folded(some):
        half = some.shape[0] // 2
        other = some[:, 64:]
        came = swap(jnp.concatenate([other[:half], other[half:]], axis=1), "zl")
        return (some[:, :64] + joined(came[:, :64], came[:, 64:])).astype(BF16)

    def block(dx, dz, first=0, count=ROWS):
        start = (((x + dx) % 4) * 4 + (zh + dz) % 4) * ROWS + first
        return start + jnp.arange(count)

    own = amplitudes
    zm, zp = to_both(own, "zh")
    own_xm, own_xp = to_both(own, "x")
    order = (jnp.arange(1024)[:, None] == source[None, :]).astype(BF16)
    columns = dot(integrals, order).astype(BF16)
    theirs, mine = columns[:, :512], columns[:, 512:]

    def paired(rows):
        return dot(rows, mine) + swap(dot(rows, theirs), "core")

    side = joined(zm, zp)
    side_xm, side_xp = to_both(side, "x")
    far = joined(shift(zp[:40], "zh", 4, -1), shift(zm[40:], "zh", 4, 1))
    early = paired(joined(own, *lax.optimization_barrier((own_xm, own_xp, side))))

    late_rows = joined(side_xm, side_xp, far)
    away = dot(late_rows, theirs)
    after_xm = joined(far, own_xm[40:], side_xm[80:])
    after_xp = joined(far, own_xp[:40], side_xp[:80])
    from_xm, from_xp = shift(after_xm, "x", 4, 1), shift(after_xp, "x", 4, -1)
    late = dot(late_rows, mine) + swap(away, "core")
    early = over_y(joined(early, late))
    from_xm, from_xp, late = lax.optimization_barrier((from_xm, from_xp, late))
    last_xm = shift(from_xm[40:80], "x", 4, 1)
    last_xp = shift(from_xp[:40], "x", 4, -1)
    rows, early = lax.optimization_barrier(
        (joined(from_xm, from_xp, last_xm, last_xp), early)
    )
    away = swap(dot(rows, theirs), "core")
    kept = lax.optimization_barrier(dot(rows, mine))
    last, early = lax.optimization_barrier((over_y_at_once(kept + away), over_zl(early)))
    sums = [early, over_zl_folded(last)]
    sites = [
        [block(0, 0), block(-1, 0), block(1, 0), block(0, -1), block(0, 1)],
        [block(-1, -1), block(-1, 1), block(1, -1), block(1, 1), block(0, 2)],
        [block(-1, 2), block(2, 0, 40, 40), block(2, 1)],
        [block(1, 2), block(2, 0, 0, 40), block(2, -1)],
        [block(2, 2, 40, 40), block(2, 2, 0, 40)],
    ]
    places = joined(*[p for ps in sites for p in ps])
    place = (places[:, None] == jnp.arange(1280)[None, :]).astype(BF16)

    def put(some, where):
        return lax.dot_general(some, where, (((0,), (0,)), ((), ())), preferred_element_type=F32)

    turned = put(sums[0], place[:800]) + put(sums[1], place[800:])
    return turned.astype(BF16)


def solution(mesh):
    split = Mesh(mesh.devices.reshape(4, 4, 4, 2, 2), ("x", "zh", "y", "zl", "core"))
    row, col = ("x", "zh"), ("y", "zl", "core")
    return jax.shard_map(
        local,
        mesh=split,
        in_specs=(P(row, col), P(col, row)),
        out_specs=P(row + col, None),
        check_vma=False,
    )
```

```python
import jax
import jax.numpy as jnp
from jax import lax
from jax.sharding import Mesh, PartitionSpec as P

ROWS = 80
F32 = jnp.float32
BF16 = jnp.bfloat16


def shift(value, axis, size, by):
    return lax.ppermute(value, axis, [(i, (i + by) % size) for i in range(size)])


def to_both(value, axis):
    return shift(value, axis, 4, 1), shift(value, axis, 4, -1)


def swap(value, axis):
    return lax.ppermute(value, axis, [(0, 1), (1, 0)])


def dot(left, right):
    return jnp.dot(left, right, preferred_element_type=F32)


def joined(*parts):
    return jnp.concatenate(parts, axis=0)


def local(amplitudes, integrals):
    x, zh, y, zl, core = (lax.axis_index(n) for n in ("x", "zh", "y", "zl", "core"))

    at = jnp.arange(1024)
    owner = jnp.where(at < 512, 1 - core, core)
    level = jnp.where(at & 64 == 0, zl, 1 - zl)
    source = ((at >> 7) & 3) * 256 + level * 128 + owner * 64 + (at & 63)

    def over_y(pair):
        split = pair.reshape(pair.shape[0], 4, 128).transpose(1, 0, 2)
        return jnp.sum(lax.all_to_all(split, "y", split_axis=0, concat_axis=0, tiled=True), axis=0)

    def over_y_at_once(pair):
        part = lambda d: lax.dynamic_slice_in_dim(pair, ((y + d) % 4) * 128, 128, axis=1)
        others = [shift(part(d), "y", 4, d) for d in (1, 3, 2)]
        return part(0) + others[0] + others[1] + others[2]

    def over_zl(some):
        return (some[:, :64] + swap(some, "zl")[:, 64:]).astype(BF16)

    def over_zl_folded(some):
        half = some.shape[0] // 2
        other = some[:, 64:]
        came = swap(jnp.concatenate([other[:half], other[half:]], axis=1), "zl")
        return (some[:, :64] + joined(came[:, :64], came[:, 64:])).astype(BF16)

    def block(dx, dz, first=0, count=ROWS):
        start = (((x + dx) % 4) * 4 + (zh + dz) % 4) * ROWS + first
        return start + jnp.arange(count)

    own = amplitudes
    zm, zp = to_both(own, "zh")
    own_xm, own_xp = to_both(own, "x")
    order = (jnp.arange(1024)[:, None] == source[None, :]).astype(BF16)
    columns = dot(integrals, order).astype(BF16)
    theirs, mine = columns[:, :512], columns[:, 512:]

    def paired(rows):
        return dot(rows, mine) + swap(dot(rows, theirs), "core")

    side = joined(zm, zp)
    side_xm, side_xp = to_both(side, "x")
    far = joined(shift(zp[:40], "zh", 4, -1), shift(zm[40:], "zh", 4, 1))
    early = paired(joined(own, *lax.optimization_barrier((own_xm, own_xp, side))))

    late_rows = joined(side_xm, side_xp, far)
    away = dot(late_rows, theirs)
    after_xm = joined(far, own_xm[40:], side_xm[80:])
    after_xp = joined(far, own_xp[:40], side_xp[:80])
    from_xm, from_xp = shift(after_xm, "x", 4, 1), shift(after_xp, "x", 4, -1)
    late = dot(late_rows, mine) + swap(away, "core")
    early = over_y(joined(early, late))
    from_xm, from_xp, late = lax.optimization_barrier((from_xm, from_xp, late))
    opposite = shift(far, "x", 4, 2)
    rows = joined(from_xm, from_xp, opposite)
    away, early = lax.optimization_barrier((dot(rows, theirs), early))
    away = swap(away, "core")
    kept = lax.optimization_barrier(dot(rows, mine))
    last, early = lax.optimization_barrier((over_y_at_once(kept + away), over_zl(early)))
    sums = [early, over_zl_folded(last)]
    sites = [
        [block(0, 0), block(-1, 0), block(1, 0), block(0, -1), block(0, 1)],
        [block(-1, -1), block(-1, 1), block(1, -1), block(1, 1), block(0, 2)],
        [block(-1, 2), block(2, 0, 40, 40), block(2, 1)],
        [block(1, 2), block(2, 0, 0, 40), block(2, -1)],
        [block(2, 2)],
    ]
    places = joined(*[p for ps in sites for p in ps])
    place = (places[:, None] == jnp.arange(1280)[None, :]).astype(BF16)

    def put(some, where):
        return lax.dot_general(some, where, (((0,), (0,)), ((), ())), preferred_element_type=F32)

    turned = put(sums[0], place[:800]) + put(sums[1], place[800:])
    return turned.astype(BF16)


def solution(mesh):
    split = Mesh(mesh.devices.reshape(4, 4, 4, 2, 2), ("x", "zh", "y", "zl", "core"))
    row, col = ("x", "zh"), ("y", "zl", "core")
    return jax.shard_map(
        local,
        mesh=split,
        in_specs=(P(row, col), P(col, row)),
        out_specs=P(row + col, None),
        check_vma=False,
    )
```

```python
import jax
import jax.numpy as jnp
from jax import lax
from jax.sharding import Mesh, PartitionSpec as P

ROWS = 80
F32 = jnp.float32
BF16 = jnp.bfloat16


def shift(value, axis, size, by):
    return lax.ppermute(value, axis, [(i, (i + by) % size) for i in range(size)])


def to_both(value, axis):
    return shift(value, axis, 4, 1), shift(value, axis, 4, -1)


def swap(value, axis):
    return lax.ppermute(value, axis, [(0, 1), (1, 0)])


def dot(left, right):
    return jnp.dot(left, right, preferred_element_type=F32)


def joined(*parts):
    return jnp.concatenate(parts, axis=0)


def local(amplitudes, integrals):
    x, zh, y, zl, core = (lax.axis_index(n) for n in ("x", "zh", "y", "zl", "core"))

    at = jnp.arange(1024)
    owner = jnp.where(at < 512, 1 - core, core)
    level = jnp.where(at & 64 == 0, zl, 1 - zl)
    source = ((at >> 7) & 3) * 256 + level * 128 + owner * 64 + (at & 63)

    def over_y(pair):
        split = pair.reshape(pair.shape[0], 4, 128).transpose(1, 0, 2)
        return jnp.sum(lax.all_to_all(split, "y", split_axis=0, concat_axis=0, tiled=True), axis=0)

    def over_y_at_once(pair):
        part = lambda d: lax.dynamic_slice_in_dim(pair, ((y + d) % 4) * 128, 128, axis=1)
        others = [shift(part(d), "y", 4, d) for d in (1, 3, 2)]
        return part(0) + others[0] + others[1] + others[2]

    def over_zl(some):
        return (some[:, :64] + swap(some, "zl")[:, 64:]).astype(BF16)

    def over_zl_folded(some):
        half = some.shape[0] // 2
        other = some[:, 64:]
        came = swap(jnp.concatenate([other[:half], other[half:]], axis=1), "zl")
        return (some[:, :64] + joined(came[:, :64], came[:, 64:])).astype(BF16)

    def block(dx, dz, first=0, count=ROWS):
        start = (((x + dx) % 4) * 4 + (zh + dz) % 4) * ROWS + first
        return start + jnp.arange(count)

    own = amplitudes
    zm, zp = to_both(own, "zh")
    own_xm, own_xp = to_both(own, "x")
    order = (jnp.arange(1024)[:, None] == source[None, :]).astype(BF16)
    columns = dot(integrals, order).astype(BF16)
    theirs, mine = columns[:, :512], columns[:, 512:]

    def paired(rows):
        return dot(rows, mine) + swap(dot(rows, theirs), "core")

    side = joined(zm, zp)
    side_xm, side_xp = to_both(side, "x")
    far = joined(shift(zp[:40], "zh", 4, -1), shift(zm[40:], "zh", 4, 1))
    early = paired(joined(own, *lax.optimization_barrier((own_xm, own_xp, side))))

    late_rows = joined(side_xm, side_xp, far)
    away = dot(late_rows, theirs)
    halves = lax.optimization_barrier((joined(far, own_xm[40:]), joined(far, own_xp[:40])))
    after_xm, after_xp = joined(halves[0], side_xm[80:]), joined(halves[1], side_xp[:80])
    from_xm, from_xp = shift(after_xm, "x", 4, 1), shift(after_xp, "x", 4, -1)
    late = dot(late_rows, mine) + swap(away, "core")
    early = over_y(joined(early, late))
    from_xm, from_xp, late = lax.optimization_barrier((from_xm, from_xp, late))
    opposite = shift(far, "x", 4, 2)
    rows = joined(from_xm, from_xp, opposite)
    away, early = lax.optimization_barrier((dot(rows, theirs), early))
    away = swap(away, "core")
    kept = lax.optimization_barrier(dot(rows, mine))
    last, early = lax.optimization_barrier((over_y_at_once(kept + away), over_zl(early)))
    sums = [early, over_zl_folded(last)]
    sites = [
        [block(0, 0), block(-1, 0), block(1, 0), block(0, -1), block(0, 1)],
        [block(-1, -1), block(-1, 1), block(1, -1), block(1, 1), block(0, 2)],
        [block(-1, 2), block(2, 0, 40, 40), block(2, 1)],
        [block(1, 2), block(2, 0, 0, 40), block(2, -1)],
        [block(2, 2)],
    ]
    places = joined(*[p for ps in sites for p in ps])
    place = (places[:, None] == jnp.arange(1280)[None, :]).astype(BF16)

    def put(some, where):
        return lax.dot_general(some, where, (((0,), (0,)), ((), ())), preferred_element_type=F32)

    turned = put(sums[0], place[:800]) + put(sums[1], place[800:])
    return turned.astype(BF16)


def solution(mesh):
    split = Mesh(mesh.devices.reshape(4, 4, 4, 2, 2), ("x", "zh", "y", "zl", "core"))
    row, col = ("x", "zh"), ("y", "zl", "core")
    return jax.shard_map(
        local,
        mesh=split,
        in_specs=(P(row, col), P(col, row)),
        out_specs=P(row + col, None),
        check_vma=False,
    )
```

```python
import jax
import jax.numpy as jnp
from jax import lax
from jax.sharding import Mesh, PartitionSpec as P

ROWS = 80
F32 = jnp.float32
BF16 = jnp.bfloat16


def shift(value, axis, size, by):
    return lax.ppermute(value, axis, [(i, (i + by) % size) for i in range(size)])


def to_both(value, axis):
    return shift(value, axis, 4, 1), shift(value, axis, 4, -1)


def swap(value, axis):
    return lax.ppermute(value, axis, [(0, 1), (1, 0)])


def dot(left, right):
    return jnp.dot(left, right, preferred_element_type=F32)


def joined(*parts):
    return jnp.concatenate(parts, axis=0)


def local(amplitudes, integrals):
    x, zh, y, zl, core = (lax.axis_index(n) for n in ("x", "zh", "y", "zl", "core"))

    at = jnp.arange(1024)
    owner = jnp.where(at < 512, 1 - core, core)
    level = jnp.where(at & 64 == 0, zl, 1 - zl)
    source = ((at >> 7) & 3) * 256 + level * 128 + owner * 64 + (at & 63)

    def over_y(pair):
        split = pair.reshape(pair.shape[0], 4, 128).transpose(1, 0, 2)
        return jnp.sum(lax.all_to_all(split, "y", split_axis=0, concat_axis=0, tiled=True), axis=0)

    def over_y_at_once(pair):
        part = lambda d: lax.dynamic_slice_in_dim(pair, ((y + d) % 4) * 128, 128, axis=1)
        others = [shift(part(d), "y", 4, d) for d in (1, 3, 2)]
        return part(0) + others[0] + others[1] + others[2]

    def over_zl(some):
        return (some[:, :64] + swap(some, "zl")[:, 64:]).astype(BF16)

    def over_zl_folded(some):
        half = some.shape[0] // 2
        other = some[:, 64:]
        came = swap(jnp.concatenate([other[:half], other[half:]], axis=1), "zl")
        return (some[:, :64] + joined(came[:, :64], came[:, 64:])).astype(BF16)

    def block(dx, dz, first=0, count=ROWS):
        start = (((x + dx) % 4) * 4 + (zh + dz) % 4) * ROWS + first
        return start + jnp.arange(count)

    own = amplitudes
    zm, zp = to_both(own, "zh")
    own_xm, own_xp = to_both(own, "x")
    order = (jnp.arange(1024)[:, None] == source[None, :]).astype(BF16)
    columns = dot(integrals, order).astype(BF16)
    theirs, mine = columns[:, :512], columns[:, 512:]

    def paired(rows):
        return dot(rows, mine) + swap(dot(rows, theirs), "core")

    side = joined(zm, zp)
    side_xm, side_xp = to_both(side, "x")
    far = joined(shift(zp[:40], "zh", 4, -1), shift(zm[40:], "zh", 4, 1))
    early = paired(joined(own, *lax.optimization_barrier((own_xm, own_xp, side))))

    late_rows = joined(side_xm, side_xp, far)
    away = dot(late_rows, theirs)
    halves = lax.optimization_barrier((joined(far, own_xm[40:]), joined(far, own_xp[:40])))
    after_xm, after_xp = joined(halves[0], side_xm[80:]), joined(halves[1], side_xp[:80])
    from_xm, from_xp = shift(after_xm, "x", 4, 1), shift(after_xp, "x", 4, -1)
    late = dot(late_rows, mine) + swap(away, "core")
    early = over_y(joined(early, late))
    from_xm, from_xp, late = lax.optimization_barrier((from_xm, from_xp, late))
    last_xm = shift(from_xm[40:80], "x", 4, 1)
    last_xp = shift(from_xp[:40], "x", 4, -1)
    rows, early = lax.optimization_barrier(
        (joined(from_xm, from_xp, last_xm, last_xp), early)
    )
    away = swap(dot(rows, theirs), "core")
    kept = lax.optimization_barrier(dot(rows, mine))
    last, early = lax.optimization_barrier((over_y_at_once(kept + away), over_zl(early)))
    sums = [early, over_zl_folded(last)]
    sites = [
        [block(0, 0), block(-1, 0), block(1, 0), block(0, -1), block(0, 1)],
        [block(-1, -1), block(-1, 1), block(1, -1), block(1, 1), block(0, 2)],
        [block(-1, 2), block(2, 0, 40, 40), block(2, 1)],
        [block(1, 2), block(2, 0, 0, 40), block(2, -1)],
        [block(2, 2, 40, 40), block(2, 2, 0, 40)],
    ]
    places = joined(*[p for ps in sites for p in ps])
    place = (places[:, None] == jnp.arange(1280)[None, :]).astype(BF16)

    def put(some, where):
        return lax.dot_general(some, where, (((0,), (0,)), ((), ())), preferred_element_type=F32)

    turned = put(sums[0], place[:800]) + put(sums[1], place[800:])
    return turned.astype(BF16)


def solution(mesh):
    split = Mesh(mesh.devices.reshape(4, 4, 4, 2, 2), ("x", "zh", "y", "zl", "core"))
    row, col = ("x", "zh"), ("y", "zl", "core")
    return jax.shard_map(
        local,
        mesh=split,
        in_specs=(P(row, col), P(col, row)),
        out_specs=P(row + col, None),
        check_vma=False,
    )
```

```python
import jax
import jax.numpy as jnp
from jax import lax
from jax.sharding import Mesh, PartitionSpec as P

ROWS = 80
F32 = jnp.float32
BF16 = jnp.bfloat16


def shift(value, axis, size, by):
    return lax.ppermute(value, axis, [(i, (i + by) % size) for i in range(size)])


def to_both(value, axis):
    return shift(value, axis, 4, 1), shift(value, axis, 4, -1)


def swap(value, axis):
    return lax.ppermute(value, axis, [(0, 1), (1, 0)])


def dot(left, right):
    return jnp.dot(left, right, preferred_element_type=F32)


def joined(*parts):
    return jnp.concatenate(parts, axis=0)


def local(amplitudes, integrals):
    x, zh, y, zl, core = (lax.axis_index(n) for n in ("x", "zh", "y", "zl", "core"))

    at = jnp.arange(1024)
    owner = jnp.where(at < 512, 1 - core, core)
    level = jnp.where(at & 64 == 0, zl, 1 - zl)
    source = ((at >> 7) & 3) * 256 + level * 128 + owner * 64 + (at & 63)

    def over_y(pair):
        split = pair.reshape(pair.shape[0], 4, 128).transpose(1, 0, 2)
        return jnp.sum(lax.all_to_all(split, "y", split_axis=0, concat_axis=0, tiled=True), axis=0)

    def over_y_at_once(pair):
        part = lambda d: lax.dynamic_slice_in_dim(pair, ((y + d) % 4) * 128, 128, axis=1)
        others = [shift(part(d), "y", 4, d) for d in (1, 3, 2)]
        return part(0) + others[0] + others[1] + others[2]

    def over_zl(some):
        return (some[:, :64] + swap(some, "zl")[:, 64:]).astype(BF16)

    def over_zl_folded(some):
        half = some.shape[0] // 2
        other = some[:, 64:]
        came = swap(jnp.concatenate([other[:half], other[half:]], axis=1), "zl")
        return (some[:, :64] + joined(came[:, :64], came[:, 64:])).astype(BF16)

    def block(dx, dz, first=0, count=ROWS):
        start = (((x + dx) % 4) * 4 + (zh + dz) % 4) * ROWS + first
        return start + jnp.arange(count)

    own = amplitudes
    zm, zp = to_both(own, "zh")
    own_xm, own_xp = to_both(own, "x")
    order = (jnp.arange(1024)[:, None] == source[None, :]).astype(BF16)
    columns = dot(integrals, order).astype(BF16)
    theirs, mine = columns[:, :512], columns[:, 512:]

    def paired(rows):
        return dot(rows, mine) + swap(dot(rows, theirs), "core")

    side = joined(zm, zp)
    side_xm, side_xp = to_both(side, "x")
    far = joined(shift(zp[:40], "zh", 4, -1), shift(zm[40:], "zh", 4, 1))
    early = paired(joined(own, *lax.optimization_barrier((own_xm, own_xp, side))))

    late_rows = joined(side_xm, side_xp, far)
    away = dot(late_rows, theirs)
    after_xm = joined(far, own_xm[40:], side_xm[80:])
    after_xp = joined(far, own_xp[:40], side_xp[:80])
    from_xm, from_xp = shift(after_xm, "x", 4, 1), shift(after_xp, "x", 4, -1)
    late = dot(late_rows, mine) + swap(away, "core")
    early = over_y(joined(early, late))
    from_xm, from_xp, late = lax.optimization_barrier((from_xm, from_xp, late))
    opposite = shift(far, "x", 4, 2)
    rows = joined(from_xm, from_xp, opposite)
    away, early = lax.optimization_barrier((dot(rows, theirs), early))
    away = swap(away, "core")
    kept = dot(rows, mine)
    last, early = lax.optimization_barrier((over_y_at_once(kept + away), over_zl(early)))
    sums = [early, over_zl_folded(last)]
    sites = [
        [block(0, 0), block(-1, 0), block(1, 0), block(0, -1), block(0, 1)],
        [block(-1, -1), block(-1, 1), block(1, -1), block(1, 1), block(0, 2)],
        [block(-1, 2), block(2, 0, 40, 40), block(2, 1)],
        [block(1, 2), block(2, 0, 0, 40), block(2, -1)],
        [block(2, 2)],
    ]
    places = joined(*[p for ps in sites for p in ps])
    place = (places[:, None] == jnp.arange(1280)[None, :]).astype(BF16)

    def put(some, where):
        return lax.dot_general(some, where, (((0,), (0,)), ((), ())), preferred_element_type=F32)

    turned = put(sums[0], place[:800]) + put(sums[1], place[800:])
    return turned.astype(BF16)


def solution(mesh):
    split = Mesh(mesh.devices.reshape(4, 4, 4, 2, 2), ("x", "zh", "y", "zl", "core"))
    row, col = ("x", "zh"), ("y", "zl", "core")
    return jax.shard_map(
        local,
        mesh=split,
        in_specs=(P(row, col), P(col, row)),
        out_specs=P(row + col, None),
        check_vma=False,
    )
```
